128 devices in a mesh: dp: 32 (over z_lo, x, y), tensor: 4 (over z_hi, core).
Axes of the slice: x: 4, y: 4, z: 4 (z_hi: 2, z_lo: 2; z = z_hi * 2 + z_lo), core: 2. Of those that a mesh axis runs over, the one named last changes fastest.
Arguments:
- hidden: bfloat16 [64, 512, 5120], P('dp'), may hold values from -5 to 5
- query_projection_matrix: bfloat16 [5120, 2560], P('dp', 'tensor'), may hold values from -0.5 to 0.5
- key_projection_matrix: bfloat16 [5120, 2560], P('dp', 'tensor'), may hold values from -0.5 to 0.5
- value_projection_matrix: bfloat16 [5120, 2560], P('dp', 'tensor'), may hold values from -0.078125 to 0.078125
- adapter_down_maps: bfloat16 [2, 8, 5120], replicated, may hold values from -0.078125 to 0.078125
- adapter_up_maps: bfloat16 [2, 8, 2560], P(None, None, 'tensor'), may hold values from -1 to 1
- cotangent: bfloat16 [64, 512, 2560], P('dp', None, 'tensor'), may hold values from -6 to 6
- lengths: int32 [64], P('dp'), may hold values from 1 to 512, 16640 in all
- random_signs_down: bfloat16 [2, 8, 5120, 4096], P(None, None, ('dp', 'tensor')), may hold values from -4 to 4
- random_signs_up: bfloat16 [2, 8, 20, 128, 4096], P(None, None, 'tensor', 'dp'), may hold values from -4 to 4
Outputs:
- features: float32 [64, 4096], P('dp', 'tensor')
The draws below stay inside these ranges and needn't reach their ends.
Inputs may be any that keep to these rules, and one draw needn't show every extreme that they name: `lengths`: positions at or beyond an example's length are padding.
All inputs are finite; a program needn't handle non-finite values. No bound on the sum of `lengths` on one device may be relied on, other than what follows from the above.
Results may differ from the reference program's by a relative error of at most 0.025.
Values may be sent and summed in bfloat16 or wider, within the bound.
A program may use at most 128 MiB of HBM per device.

```python
import math
import jax
import jax.numpy as jnp
import numpy as np
from jax import lax

MODEL_DIM = 5120
HEAD_DIM = 128
TRAINED_HEADS = 20
ADAPTER_RANK = 8
FEAT = 4096
POOL_LENGTH = 512
EXAMPLES = 64


def channel_pattern(key):
    stride = MODEL_DIM // 16
    offset = jax.random.randint(jax.random.fold_in(key, 101), (), 0, stride)
    sign_picks = jax.random.randint(jax.random.fold_in(key, 103), (MODEL_DIM,), 0, 2)
    chosen = jnp.arange(MODEL_DIM) % stride == offset
    pattern = jnp.where(chosen, (sign_picks * 2 - 1).astype(jnp.float32), jnp.zeros((MODEL_DIM,), jnp.float32))
    return (pattern, chosen)


def drawn_weight(key, salt_value):
    pattern, chosen = channel_pattern(key)
    full_shape = (MODEL_DIM, TRAINED_HEADS * HEAD_DIM)
    noise_key = jax.random.fold_in(key, salt_value)
    base_part = jnp.clip(jax.random.normal(noise_key, full_shape, jnp.float32), -4.0, 4.0)
    columns = jnp.arange(TRAINED_HEADS * HEAD_DIM) % HEAD_DIM
    slow_pairs = (columns % (HEAD_DIM // 2) >= HEAD_DIM // 2 - 8).astype(jnp.float32)
    strength = (14.0 * HEAD_DIM ** 0.5 / 4096.0) ** 0.5
    return (base_part * MODEL_DIM ** (-0.5) + strength * pattern[:, None] * slow_pairs[None, :]).astype(jnp.bfloat16)


def draw_query_projection_matrix(key, part):
    return drawn_weight(key, 211)


def draw_key_projection_matrix(key, part):
    return drawn_weight(key, 223)


def draw_hidden(key, part):
    pattern, chosen = channel_pattern(key)
    full_shape = (EXAMPLES, POOL_LENGTH, MODEL_DIM)
    noise_key = jax.random.fold_in(key, 227)
    noise_part = jnp.clip(jax.random.normal(noise_key, full_shape, jnp.float32), -5.0, 5.0)
    quiet_part = jnp.where(chosen[None, None, :], 0.3 * noise_part, noise_part)
    positions = jnp.arange(POOL_LENGTH)[None, :]
    marked = jax.random.randint(jax.random.fold_in(key, 233), (EXAMPLES, POOL_LENGTH), 0, 32) == 0
    sink_rows = marked | (positions == 0)
    levels = jax.random.uniform(jax.random.fold_in(key, 239), (EXAMPLES, POOL_LENGTH), jnp.float32, 1.5, 5.0)
    levels = jnp.where(positions == 0, 5.0, levels)
    sink_values = levels[:, :, None] * pattern[None, None, :]
    placed = sink_rows[:, :, None] & chosen[None, None, :]
    return jnp.where(placed, sink_values, quiet_part).astype(jnp.bfloat16)


def column_weights():
    steps = jnp.arange(FEAT, dtype=jnp.float32) / (FEAT - 1)
    return jnp.exp(steps * 1.0986123)


def signed_table(key, salt_value, shape):
    sign_key = jax.random.fold_in(key, salt_value)
    picks = jax.random.randint(sign_key, shape, 0, 2)
    entries = (picks * 2 - 1).astype(jnp.float32)
    return (entries * column_weights()).astype(jnp.bfloat16)


def draw_random_signs_down(key, part):
    return signed_table(key, 11, (2, ADAPTER_RANK, MODEL_DIM, FEAT))


def draw_random_signs_up(key, part):
    return signed_table(key, 23, (2, ADAPTER_RANK, TRAINED_HEADS, HEAD_DIM, FEAT))


def shard_levels(own_key, extent, cuts, smallest, top_value):
    loudness, own = 1.0, jax.random.fold_in(own_key, 6)
    for position, shards_of in cuts:
        draws = jnp.exp(jax.random.uniform(jax.random.fold_in(own, position), (shards_of,), jnp.float32, smallest / len(cuts), top_value / len(cuts)))
        loudness = loudness * jnp.repeat(draws, extent[position] // shards_of).reshape([-1 if axis == position else 1 for axis in range(len(extent))])
    return loudness


def length_profile(amount, total, reach, skew):
    loads = [(1 << 20) // math.isqrt(standing ** skew) + 1 for standing in range(2, amount + 1)]
    surplus, holding = total - reach - (amount - 1), [1] * (amount - 1)
    while surplus > 0:
        free = [i for i in range(amount - 1) if holding[i] < reach]
        pool, budget = sum([loads[i] for i in free]), surplus
        for i in free:
            more = min(reach - holding[i], max(1, budget * loads[i] // pool), surplus)
            holding[i] = holding[i] + more
            surplus = surplus - more
    return np.array([reach] + holding)


def uneven(own_key, number_of, total, reach, skew):
    if number_of == 2:
        one = jax.random.randint(own_key, (), max(1, total - reach), min(reach, total - 1) + 1)
        return jnp.stack([one, total - one])
    sizes = jnp.asarray(length_profile(number_of, total, reach, skew), jnp.int32)
    couples = (number_of - 1) // 2
    giver, sink = sizes[1:1 + 2 * couples:2], sizes[2:2 + 2 * couples:2]
    margin = jnp.minimum(giver - 1, reach - sink)
    passed = jax.random.randint(jax.random.fold_in(own_key, 1), (couples,), 0, 1 << 20) % (margin + 1)
    sizes = sizes.at[1:1 + 2 * couples:2].set(giver - passed).at[2:2 + 2 * couples:2].set(sink + passed)
    return sizes[jax.random.permutation(jax.random.fold_in(own_key, 2), number_of)]


def centred(rng, shape, spread, bound, pieces=(), kind=jnp.bfloat16):
    loudness = shard_levels(rng, shape, pieces, -0.22, 0.18) if pieces else 1.0
    values = jax.random.normal(rng, shape, jnp.float32) * spread * loudness
    return jnp.minimum(jnp.maximum(values, -bound), bound).astype(kind)


def setup_inputs(seed: int = 0) -> dict:
    keys = jax.random.split(jax.random.key(seed), 11)
    hidden = draw_hidden(jax.random.fold_in(keys[10], 71), 0)
    query_projection_matrix = draw_query_projection_matrix(jax.random.fold_in(keys[10], 71), 0)
    key_projection_matrix = draw_key_projection_matrix(jax.random.fold_in(keys[10], 71), 0)
    value_projection_matrix = centred(keys[3], (MODEL_DIM, TRAINED_HEADS * HEAD_DIM), MODEL_DIM ** -0.5, 0.078125, ((0, 32), (1, 4)))
    adapter_down_maps = centred(keys[4], (2, ADAPTER_RANK, MODEL_DIM), MODEL_DIM ** -0.5, 0.078125)
    adapter_up_maps = centred(keys[5], (2, ADAPTER_RANK, TRAINED_HEADS * HEAD_DIM), (4 * ADAPTER_RANK) ** -0.5, 1.0, ((2, 4),))
    cotangent = centred(keys[6], (EXAMPLES, POOL_LENGTH, TRAINED_HEADS * HEAD_DIM), 1.0, 6.0, ((0, 32), (2, 4)))
    lengths = uneven(keys[7], EXAMPLES, EXAMPLES * POOL_LENGTH // 2 + POOL_LENGTH // 2, POOL_LENGTH, 2).astype(jnp.int32)
    random_signs_down = draw_random_signs_down(jax.random.fold_in(keys[10], 71), 0)
    random_signs_up = draw_random_signs_up(jax.random.fold_in(keys[10], 71), 0)
    return dict(hidden=hidden, query_projection_matrix=query_projection_matrix, key_projection_matrix=key_projection_matrix, value_projection_matrix=value_projection_matrix, adapter_down_maps=adapter_down_maps, adapter_up_maps=adapter_up_maps, cotangent=cotangent, lengths=lengths, random_signs_down=random_signs_down, random_signs_up=random_signs_up)


adapter_scale = 2.0
rope_base = 10000.0
norm_eps = 1e-05
masked_score = -1e+30

def rope_tables(seq_len, head_width):
    half_width = head_width // 2
    frequency = rope_base ** (-2.0 * jnp.arange(half_width, dtype=jnp.float32) / head_width)
    angles = jnp.arange(seq_len, dtype=jnp.float32)[:, None] * frequency[None, :]
    rotary_cosines = jnp.concatenate([jnp.cos(angles), jnp.cos(angles)], axis=1)
    rotary_sines = jnp.concatenate([jnp.sin(angles), jnp.sin(angles)], axis=1)
    return (rotary_cosines, rotary_sines)

def apply_rotary(tensor_in, rotary_cosines, rotary_sines):
    half_width = tensor_in.shape[-1] // 2
    turned = jnp.concatenate([-tensor_in[..., half_width:], tensor_in[..., :half_width]], axis=-1)
    return tensor_in * rotary_cosines[:, None, :] + turned * rotary_sines[:, None, :]

def unrotate(gradient, rotary_cosines, rotary_sines):
    half_width = gradient.shape[-1] // 2
    scaled = gradient * rotary_sines[:, None, :]
    rotated_back = jnp.concatenate([scaled[..., half_width:], -scaled[..., :half_width]], axis=-1)
    return gradient * rotary_cosines[:, None, :] + rotated_back

def attention_grads(query_per_head, key_heads, value_per_head, grad_out, seq_length):
    seq_len = query_per_head.shape[0]
    inv_root = query_per_head.shape[-1] ** (-0.5)
    key_wide = key_heads.astype(jnp.float32)
    scores = jnp.einsum('qhc,khc->hqk', query_per_head.astype(jnp.float32), key_wide) * inv_root
    query_pos = jnp.arange(seq_len, dtype=jnp.int32)[:, None]
    key_pos = jnp.arange(seq_len, dtype=jnp.int32)[None, :]
    allowed = (key_pos <= query_pos) & (key_pos < seq_length)
    scores = jnp.where(allowed[None], scores, masked_score)
    row_max = lax.optimization_barrier(jnp.max(scores, axis=-1, keepdims=True))
    expon = jnp.exp(scores - row_max)
    attention = expon / lax.optimization_barrier(jnp.sum(expon, axis=-1, keepdims=True))
    attention_low = attention.astype(jnp.bfloat16)
    grad_wide = grad_out.astype(jnp.float32)
    grad_values = jnp.einsum('hqk,qhc->khc', attention_low.astype(jnp.float32), grad_wide)
    grad_attention = jnp.einsum('qhc,khc->hqk', grad_wide, value_per_head.astype(jnp.float32))
    inner_sum = lax.optimization_barrier(jnp.sum(attention * grad_attention, axis=-1, keepdims=True))
    grad_scores = (attention * (grad_attention - inner_sum)).astype(jnp.bfloat16)
    grad_query = jnp.einsum('hqk,khc->qhc', grad_scores.astype(jnp.float32), key_wide) * inv_root
    return (grad_query, grad_values)

def reference(hidden, query_projection_matrix, key_projection_matrix, value_projection_matrix, adapter_down_maps, adapter_up_maps, cotangent, lengths, random_signs_down, random_signs_up):
    rotary_cosines, rotary_sines = rope_tables(POOL_LENGTH, HEAD_DIM)
    query_wide = query_projection_matrix.astype(jnp.float32)
    key_wide = key_projection_matrix.astype(jnp.float32)
    value_wide = value_projection_matrix.astype(jnp.float32)
    down_map_full = adapter_down_maps.astype(jnp.float32)
    up_map_full = adapter_up_maps.astype(jnp.float32)
    top_precision = lax.Precision.HIGHEST

    def per_example(example):
        sequence, grad_out, seq_length = example
        sequence_full = sequence.astype(jnp.float32)
        inner_hidden = jnp.einsum('no,wio->nwi', sequence_full, down_map_full, precision=top_precision).astype(jnp.bfloat16)
        raised_features = jnp.einsum('kdg,dgj->kdj', inner_hidden.astype(jnp.float32), up_map_full, precision=top_precision)
        plain_query = jnp.dot(sequence_full, query_wide, precision=top_precision)
        base_key = jnp.dot(sequence_full, key_wide, precision=top_precision)
        plain_value = jnp.dot(sequence_full, value_wide, precision=top_precision)
        query_per_head = apply_rotary((plain_query + adapter_scale * raised_features[:, 0]).reshape(POOL_LENGTH, TRAINED_HEADS, HEAD_DIM), rotary_cosines, rotary_sines).astype(jnp.bfloat16)
        key_heads = apply_rotary(base_key.reshape(POOL_LENGTH, TRAINED_HEADS, HEAD_DIM), rotary_cosines, rotary_sines).astype(jnp.bfloat16)
        value_per_head = (plain_value + adapter_scale * raised_features[:, 1]).astype(jnp.bfloat16).reshape(POOL_LENGTH, TRAINED_HEADS, HEAD_DIM)
        valid = jnp.arange(POOL_LENGTH, dtype=jnp.int32) < seq_length
        masked_out = jnp.where(valid[:, None], grad_out, jnp.zeros_like(grad_out)).reshape(POOL_LENGTH, TRAINED_HEADS, HEAD_DIM)
        grad_query, grad_values = attention_grads(query_per_head, key_heads, value_per_head, masked_out, seq_length)
        grad_query = unrotate(grad_query, rotary_cosines, rotary_sines).astype(jnp.bfloat16).reshape(POOL_LENGTH, TRAINED_HEADS * HEAD_DIM)
        grad_values = grad_values.astype(jnp.bfloat16).reshape(POOL_LENGTH, TRAINED_HEADS * HEAD_DIM)
        per_head_gradient = jnp.stack([grad_query, grad_values], axis=1).astype(jnp.float32)
        adapter_branch = jnp.einsum('qvk,vnk->qvn', per_head_gradient, up_map_full, precision=top_precision).astype(jnp.bfloat16)
        down_map_gradient = adapter_scale * jnp.einsum('hzj,hb->zjb', adapter_branch.astype(jnp.float32), sequence_full, precision=top_precision)
        up_map_gradient = adapter_scale * jnp.einsum('huz,hue->uze', inner_hidden.astype(jnp.float32), per_head_gradient, precision=top_precision)
        return (down_map_gradient, up_map_gradient)
    down_map_gradient, up_map_gradient = lax.map(per_example, (hidden, cotangent, lengths))
    down_low = down_map_gradient.astype(jnp.bfloat16).reshape(EXAMPLES, 2 * ADAPTER_RANK * MODEL_DIM)
    up_low = up_map_gradient.astype(jnp.bfloat16).reshape(EXAMPLES, 2 * ADAPTER_RANK * TRAINED_HEADS * HEAD_DIM)
    down_table = random_signs_down.reshape(2 * ADAPTER_RANK * MODEL_DIM, FEAT)
    up_table = random_signs_up.reshape(2 * ADAPTER_RANK * TRAINED_HEADS * HEAD_DIM, FEAT)
    raw = jnp.dot(down_low, down_table, preferred_element_type=jnp.float32) + jnp.dot(up_low, up_table, preferred_element_type=jnp.float32)
    mean_square = lax.optimization_barrier(jnp.mean(raw * raw, axis=1, keepdims=True))
    return raw * lax.rsqrt(mean_square + norm_eps)
```

```python
import jax
import jax.numpy as jnp
from jax import lax
from jax.sharding import PartitionSpec as P

HEAD_DIM = 128
ADAPTER_RANK = 8
FEAT = 4096


adapter_scale = 2.0
rope_base = 10000.0
norm_eps = 1e-05
masked_score = -1e30


def rope_tables(seq_len, head_width):
    half_width = head_width // 2
    frequency = rope_base ** (-2.0 * jnp.arange(half_width, dtype=jnp.float32) / head_width)
    angles = jnp.arange(seq_len, dtype=jnp.float32)[:, None] * frequency[None, :]
    rotary_cosines = jnp.concatenate([jnp.cos(angles), jnp.cos(angles)], axis=1)
    rotary_sines = jnp.concatenate([jnp.sin(angles), jnp.sin(angles)], axis=1)
    return (rotary_cosines, rotary_sines)


def apply_rotary(tensor_in, rotary_cosines, rotary_sines):
    half_width = tensor_in.shape[-1] // 2
    turned = jnp.concatenate([-tensor_in[..., half_width:], tensor_in[..., :half_width]], axis=-1)
    return tensor_in * rotary_cosines[:, None, :] + turned * rotary_sines[:, None, :]


def unrotate(gradient, rotary_cosines, rotary_sines):
    half_width = gradient.shape[-1] // 2
    scaled = gradient * rotary_sines[:, None, :]
    rotated_back = jnp.concatenate([scaled[..., half_width:], -scaled[..., :half_width]], axis=-1)
    return gradient * rotary_cosines[:, None, :] + rotated_back


def attention_grads(example):
    query_per_head, key_heads, value_per_head, grad_out, seq_length = example
    seq_len = query_per_head.shape[0]
    inv_root = query_per_head.shape[-1] ** (-0.5)
    scores = (
        jnp.einsum("qhc,khc->hqk", query_per_head, key_heads, preferred_element_type=jnp.float32)
        * inv_root
    )
    query_pos = jnp.arange(seq_len, dtype=jnp.int32)[:, None]
    key_pos = jnp.arange(seq_len, dtype=jnp.int32)[None, :]
    allowed = (key_pos <= query_pos) & (key_pos < seq_length)
    scores = jnp.where(allowed[None], scores, masked_score)
    row_max = jnp.max(scores, axis=-1, keepdims=True)
    expon = jnp.exp(scores - row_max)
    attention = expon / jnp.sum(expon, axis=-1, keepdims=True)
    attention_low = attention.astype(jnp.bfloat16)
    grad_values = jnp.einsum(
        "hqk,qhc->khc", attention_low, grad_out, preferred_element_type=jnp.float32
    )
    grad_attention = jnp.einsum(
        "qhc,khc->hqk", grad_out, value_per_head, preferred_element_type=jnp.float32
    )
    inner_sum = jnp.sum(attention * grad_attention, axis=-1, keepdims=True)
    grad_scores = (attention * (grad_attention - inner_sum)).astype(jnp.bfloat16)
    grad_query = (
        jnp.einsum("hqk,khc->qhc", grad_scores, key_heads, preferred_element_type=jnp.float32)
        * inv_root
    )
    return (grad_query, grad_values)


def body(
    hidden,
    query_projection_matrix,
    key_projection_matrix,
    value_projection_matrix,
    adapter_down_maps,
    adapter_up_maps,
    cotangent,
    lengths,
    random_signs_down,
    random_signs_up,
):
    seq_count, seq_len, model_width = hidden.shape
    local_cols = query_projection_matrix.shape[1]
    heads_local = local_cols // HEAD_DIM
    token_matrix = hidden.reshape(seq_count * seq_len, model_width)

    def add_rows(weight_piece):
        return jnp.dot(token_matrix, weight_piece, preferred_element_type=jnp.float32)

    parts_dp = lax.axis_size("dp")
    local_rows = jnp.concatenate(
        [query_projection_matrix, key_projection_matrix, value_projection_matrix], axis=1
    )
    copies = jnp.broadcast_to(local_rows[None], (parts_dp,) + local_rows.shape)
    all_rows = lax.all_to_all(copies, "dp", 0, 0, tiled=True).reshape(
        parts_dp * local_rows.shape[0], local_rows.shape[1]
    )
    projected = add_rows(all_rows)
    plain_query = projected[:, :local_cols]
    base_key = projected[:, local_cols : 2 * local_cols]
    plain_value = projected[:, 2 * local_cols :]
    rotary_cosines, rotary_sines = rope_tables(seq_len, HEAD_DIM)
    inner_hidden = jnp.einsum(
        "no,wio->nwi", token_matrix, adapter_down_maps, preferred_element_type=jnp.float32
    ).astype(jnp.bfloat16)
    raised_features = jnp.einsum(
        "kdg,dgj->kdj", inner_hidden, adapter_up_maps, preferred_element_type=jnp.float32
    )
    head_layout = (seq_count, seq_len, heads_local, HEAD_DIM)
    query_per_head = apply_rotary(
        (plain_query + adapter_scale * raised_features[:, 0]).reshape(head_layout),
        rotary_cosines,
        rotary_sines,
    ).astype(jnp.bfloat16)
    key_heads = apply_rotary(base_key.reshape(head_layout), rotary_cosines, rotary_sines).astype(
        jnp.bfloat16
    )
    value_per_head = (
        (plain_value + adapter_scale * raised_features[:, 1])
        .astype(jnp.bfloat16)
        .reshape(head_layout)
    )
    valid = jnp.arange(seq_len, dtype=jnp.int32)[None, :] < lengths[:, None]
    masked_out = jnp.where(valid[:, :, None], cotangent, jnp.zeros_like(cotangent)).reshape(
        head_layout
    )
    grad_query, grad_values = lax.map(
        attention_grads, (query_per_head, key_heads, value_per_head, masked_out, lengths)
    )
    grad_query = (
        unrotate(grad_query, rotary_cosines, rotary_sines)
        .astype(jnp.bfloat16)
        .reshape(seq_count, seq_len, local_cols)
    )
    grad_values = grad_values.astype(jnp.bfloat16).reshape(seq_count, seq_len, local_cols)
    per_head_gradient = jnp.stack([grad_query, grad_values], axis=2)
    branch_portion = jnp.einsum(
        "liov,ohv->lioh", per_head_gradient, adapter_up_maps, preferred_element_type=jnp.float32
    )
    adapter_branch = lax.psum(branch_portion, "tensor").astype(jnp.bfloat16)
    middle_seq = inner_hidden.reshape(seq_count, seq_len, 2, ADAPTER_RANK)
    up_map_gradient = adapter_scale * jnp.einsum(
        "esar,esac->earc", middle_seq, per_head_gradient, preferred_element_type=jnp.float32
    )
    parts_tensor = lax.axis_size("tensor")
    row_block = model_width // (parts_dp * parts_tensor)
    hidden_blocks = hidden.reshape(seq_count, seq_len, parts_dp, parts_tensor, row_block)
    local_column_range = lax.dynamic_index_in_dim(
        hidden_blocks, lax.axis_index("tensor"), axis=3, keepdims=False
    )
    down_map_local = adapter_scale * jnp.einsum(
        "ykzu,ykhc->yhzuc", adapter_branch, local_column_range, preferred_element_type=jnp.float32
    )
    down_map_local = down_map_local.reshape(seq_count, parts_dp, 1, 2 * ADAPTER_RANK * row_block)
    slice_len = HEAD_DIM // parts_dp
    up_blocks = up_map_gradient.reshape(
        seq_count, 2, ADAPTER_RANK, heads_local, parts_dp, slice_len
    )
    up_blocks = up_blocks.transpose(0, 4, 1, 2, 3, 5).reshape(
        seq_count, parts_dp, 1, 2 * ADAPTER_RANK * heads_local * slice_len
    )
    packed = jnp.concatenate([down_map_local, up_blocks], axis=3).astype(jnp.bfloat16)
    routed = lax.all_to_all(packed, "dp", split_axis=1, concat_axis=0, tiled=True)
    gathered = routed.reshape(routed.shape[0], routed.shape[3])
    down_count = down_map_local.shape[3]
    down_table = random_signs_down.reshape(down_count, random_signs_down.shape[-1])
    up_table = random_signs_up.reshape(gathered.shape[1] - down_count, random_signs_up.shape[-1])
    partial = (
        jnp.dot(gathered[:, :down_count], down_table, preferred_element_type=jnp.float32)
        + jnp.dot(gathered[:, down_count:], up_table, preferred_element_type=jnp.float32)
    ).astype(jnp.bfloat16)
    own_count = partial.shape[0] // parts_dp
    to_owner = lax.all_to_all(
        partial.reshape(parts_dp, own_count, partial.shape[1]), "dp", 0, 0, tiled=True
    )
    own_rows = jnp.sum(to_owner.astype(jnp.float32), axis=0)
    feat_block = own_rows.shape[1] // parts_tensor
    to_block = lax.all_to_all(
        own_rows.reshape(own_count, parts_tensor, feat_block), "tensor", 1, 1, tiled=True
    )
    features_local = jnp.sum(to_block, axis=1)
    squares = lax.psum(jnp.sum(features_local * features_local, axis=1), "tensor")
    return features_local * lax.rsqrt(squares / FEAT + norm_eps)[:, None]


def solution(mesh):
    return jax.shard_map(
        body,
        mesh=mesh,
        in_specs=(
            P("dp", None, None),
            P("dp", "tensor"),
            P("dp", "tensor"),
            P("dp", "tensor"),
            P(),
            P(None, None, "tensor"),
            P("dp", None, "tensor"),
            P("dp"),
            P(None, None, ("dp", "tensor"), None),
            P(None, None, "tensor", "dp", None),
        ),
        out_specs=P("dp", "tensor"),
        check_vma=False,
    )
```

```python
import jax
import jax.numpy as jnp
from jax import lax
from jax.sharding import PartitionSpec as P

HEAD_DIM = 128
ADAPTER_RANK = 8
FEAT = 4096


adapter_scale = 2.0
rope_base = 10000.0
norm_eps = 1e-05
masked_score = -1e30


def rope_tables(seq_len, head_width):
    half_width = head_width // 2
    frequency = rope_base ** (-2.0 * jnp.arange(half_width, dtype=jnp.float32) / head_width)
    angles = jnp.arange(seq_len, dtype=jnp.float32)[:, None] * frequency[None, :]
    rotary_cosines = jnp.concatenate([jnp.cos(angles), jnp.cos(angles)], axis=1)
    rotary_sines = jnp.concatenate([jnp.sin(angles), jnp.sin(angles)], axis=1)
    return (rotary_cosines, rotary_sines)


def apply_rotary(tensor_in, rotary_cosines, rotary_sines):
    half_width = tensor_in.shape[-1] // 2
    turned = jnp.concatenate([-tensor_in[..., half_width:], tensor_in[..., :half_width]], axis=-1)
    return tensor_in * rotary_cosines[:, None, :] + turned * rotary_sines[:, None, :]


def unrotate(gradient, rotary_cosines, rotary_sines):
    half_width = gradient.shape[-1] // 2
    scaled = gradient * rotary_sines[:, None, :]
    rotated_back = jnp.concatenate([scaled[..., half_width:], -scaled[..., :half_width]], axis=-1)
    return gradient * rotary_cosines[:, None, :] + rotated_back


def attention_grads(example):
    query_per_head, key_heads, value_per_head, grad_out, seq_length = example
    seq_len = query_per_head.shape[0]
    inv_root = query_per_head.shape[-1] ** (-0.5)
    scores = (
        jnp.einsum("qhc,khc->hqk", query_per_head, key_heads, preferred_element_type=jnp.float32)
        * inv_root
    )
    query_pos = jnp.arange(seq_len, dtype=jnp.int32)[:, None]
    key_pos = jnp.arange(seq_len, dtype=jnp.int32)[None, :]
    allowed = (key_pos <= query_pos) & (key_pos < seq_length)
    scores = jnp.where(allowed[None], scores, masked_score)
    row_max = jnp.max(scores, axis=-1, keepdims=True)
    expon = jnp.exp(scores - row_max)
    attention = expon / jnp.sum(expon, axis=-1, keepdims=True)
    attention_low = attention.astype(jnp.bfloat16)
    grad_values = jnp.einsum(
        "hqk,qhc->khc", attention_low, grad_out, preferred_element_type=jnp.float32
    )
    grad_attention = jnp.einsum(
        "qhc,khc->hqk", grad_out, value_per_head, preferred_element_type=jnp.float32
    )
    inner_sum = jnp.sum(attention * grad_attention, axis=-1, keepdims=True)
    grad_scores = (attention * (grad_attention - inner_sum)).astype(jnp.bfloat16)
    grad_query = (
        jnp.einsum("hqk,khc->qhc", grad_scores, key_heads, preferred_element_type=jnp.float32)
        * inv_root
    )
    return (grad_query, grad_values)


def body(
    hidden,
    query_projection_matrix,
    key_projection_matrix,
    value_projection_matrix,
    adapter_down_maps,
    adapter_up_maps,
    cotangent,
    lengths,
    random_signs_down,
    random_signs_up,
):
    seq_count, seq_len, model_width = hidden.shape
    local_cols = query_projection_matrix.shape[1]
    heads_local = local_cols // HEAD_DIM
    token_matrix = hidden.reshape(seq_count * seq_len, model_width)

    def add_rows(weight_piece):
        return jnp.dot(token_matrix, weight_piece, preferred_element_type=jnp.float32)

    parts_dp = lax.axis_size("dp")
    local_rows = jnp.concatenate(
        [query_projection_matrix, key_projection_matrix, value_projection_matrix], axis=1
    )
    all_rows = lax.all_gather(local_rows, "dp", axis=0, tiled=True)
    projected = add_rows(all_rows)
    plain_query = projected[:, :local_cols]
    base_key = projected[:, local_cols : 2 * local_cols]
    plain_value = projected[:, 2 * local_cols :]
    rotary_cosines, rotary_sines = rope_tables(seq_len, HEAD_DIM)
    inner_hidden = jnp.einsum(
        "no,wio->nwi", token_matrix, adapter_down_maps, preferred_element_type=jnp.float32
    ).astype(jnp.bfloat16)
    raised_features = jnp.einsum(
        "kdg,dgj->kdj", inner_hidden, adapter_up_maps, preferred_element_type=jnp.float32
    )
    head_layout = (seq_count, seq_len, heads_local, HEAD_DIM)
    query_per_head = apply_rotary(
        (plain_query + adapter_scale * raised_features[:, 0]).reshape(head_layout),
        rotary_cosines,
        rotary_sines,
    ).astype(jnp.bfloat16)
    key_heads = apply_rotary(base_key.reshape(head_layout), rotary_cosines, rotary_sines).astype(
        jnp.bfloat16
    )
    value_per_head = (
        (plain_value + adapter_scale * raised_features[:, 1])
        .astype(jnp.bfloat16)
        .reshape(head_layout)
    )
    valid = jnp.arange(seq_len, dtype=jnp.int32)[None, :] < lengths[:, None]
    masked_out = jnp.where(valid[:, :, None], cotangent, jnp.zeros_like(cotangent)).reshape(
        head_layout
    )
    grad_query, grad_values = lax.map(
        attention_grads, (query_per_head, key_heads, value_per_head, masked_out, lengths)
    )
    grad_query = (
        unrotate(grad_query, rotary_cosines, rotary_sines)
        .astype(jnp.bfloat16)
        .reshape(seq_count, seq_len, local_cols)
    )
    grad_values = grad_values.astype(jnp.bfloat16).reshape(seq_count, seq_len, local_cols)
    per_head_gradient = jnp.stack([grad_query, grad_values], axis=2)
    branch_portion = jnp.einsum(
        "liov,ohv->lioh", per_head_gradient, adapter_up_maps, preferred_element_type=jnp.float32
    )
    adapter_branch = lax.psum(branch_portion, "tensor").astype(jnp.bfloat16)
    middle_seq = inner_hidden.reshape(seq_count, seq_len, 2, ADAPTER_RANK)
    up_map_gradient = adapter_scale * jnp.einsum(
        "esar,esac->earc", middle_seq, per_head_gradient, preferred_element_type=jnp.float32
    )
    parts_tensor = lax.axis_size("tensor")
    row_block = model_width // (parts_dp * parts_tensor)
    hidden_blocks = hidden.reshape(seq_count, seq_len, parts_dp, parts_tensor, row_block)
    local_column_range = lax.dynamic_index_in_dim(
        hidden_blocks, lax.axis_index("tensor"), axis=3, keepdims=False
    )
    down_map_local = adapter_scale * jnp.einsum(
        "ykzu,ykhc->yhzuc", adapter_branch, local_column_range, preferred_element_type=jnp.float32
    )
    down_map_local = down_map_local.reshape(seq_count, parts_dp, 1, 2 * ADAPTER_RANK * row_block)
    slice_len = HEAD_DIM // parts_dp
    up_blocks = up_map_gradient.reshape(
        seq_count, 2, ADAPTER_RANK, heads_local, parts_dp, slice_len
    )
    up_blocks = up_blocks.transpose(0, 4, 1, 2, 3, 5).reshape(
        seq_count, parts_dp, 1, 2 * ADAPTER_RANK * heads_local * slice_len
    )
    packed = jnp.concatenate([down_map_local, up_blocks], axis=3).astype(jnp.bfloat16)
    routed = lax.all_to_all(packed, "dp", split_axis=1, concat_axis=0, tiled=True)
    gathered = routed.reshape(routed.shape[0], routed.shape[3])
    down_count = down_map_local.shape[3]
    down_table = random_signs_down.reshape(down_count, random_signs_down.shape[-1])
    up_table = random_signs_up.reshape(gathered.shape[1] - down_count, random_signs_up.shape[-1])
    partial = (
        jnp.dot(gathered[:, :down_count], down_table, preferred_element_type=jnp.float32)
        + jnp.dot(gathered[:, down_count:], up_table, preferred_element_type=jnp.float32)
    ).astype(jnp.bfloat16)
    own_count = partial.shape[0] // parts_dp
    to_owner = lax.all_to_all(
        partial.reshape(parts_dp, own_count, partial.shape[1]), "dp", 0, 0, tiled=True
    )
    own_rows = jnp.sum(to_owner.astype(jnp.float32), axis=0)
    feat_block = own_rows.shape[1] // parts_tensor
    full_rows = lax.psum(own_rows, "tensor")
    squares = jnp.sum(full_rows * full_rows, axis=1)
    features_local = lax.dynamic_slice_in_dim(
        full_rows, lax.axis_index("tensor") * feat_block, feat_block, axis=1
    )
    return features_local * lax.rsqrt(squares / FEAT + norm_eps)[:, None]


def solution(mesh):
    return jax.shard_map(
        body,
        mesh=mesh,
        in_specs=(
            P("dp", None, None),
            P("dp", "tensor"),
            P("dp", "tensor"),
            P("dp", "tensor"),
            P(),
            P(None, None, "tensor"),
            P("dp", None, "tensor"),
            P("dp"),
            P(None, None, ("dp", "tensor"), None),
            P(None, None, "tensor", "dp", None),
        ),
        out_specs=P("dp", "tensor"),
        check_vma=False,
    )
```

```python
import jax
import jax.numpy as jnp
from jax import lax
from jax.sharding import Mesh, PartitionSpec as P

HEAD_DIM = 128
ADAPTER_RANK = 8
FEAT = 4096
DP_AXES = ("zl", "x", "y")
TP_AXES = ("zh", "core")


adapter_scale = 2.0
rope_base = 10000.0
norm_eps = 1e-05
masked_score = -1e30


def rope_tables(seq_len, head_width):
    half_width = head_width // 2
    frequency = rope_base ** (-2.0 * jnp.arange(half_width, dtype=jnp.float32) / head_width)
    angles = jnp.arange(seq_len, dtype=jnp.float32)[:, None] * frequency[None, :]
    rotary_cosines = jnp.concatenate([jnp.cos(angles), jnp.cos(angles)], axis=1)
    rotary_sines = jnp.concatenate([jnp.sin(angles), jnp.sin(angles)], axis=1)
    return (rotary_cosines, rotary_sines)


def apply_rotary(tensor_in, rotary_cosines, rotary_sines):
    half_width = tensor_in.shape[-1] // 2
    turned = jnp.concatenate([-tensor_in[..., half_width:], tensor_in[..., :half_width]], axis=-1)
    return tensor_in * rotary_cosines[:, None, :] + turned * rotary_sines[:, None, :]


def unrotate(gradient, rotary_cosines, rotary_sines):
    half_width = gradient.shape[-1] // 2
    scaled = gradient * rotary_sines[:, None, :]
    rotated_back = jnp.concatenate([scaled[..., half_width:], -scaled[..., :half_width]], axis=-1)
    return gradient * rotary_cosines[:, None, :] + rotated_back


def attention_grads(example):
    query_per_head, key_heads, value_per_head, grad_out, seq_length = example
    seq_len = query_per_head.shape[0]
    inv_root = query_per_head.shape[-1] ** (-0.5)
    scores = (
        jnp.einsum("qhc,khc->hqk", query_per_head, key_heads, preferred_element_type=jnp.float32)
        * inv_root
    )
    query_pos = jnp.arange(seq_len, dtype=jnp.int32)[:, None]
    key_pos = jnp.arange(seq_len, dtype=jnp.int32)[None, :]
    allowed = (key_pos <= query_pos) & (key_pos < seq_length)
    scores = jnp.where(allowed[None], scores, masked_score)
    row_max = jnp.max(scores, axis=-1, keepdims=True)
    expon = jnp.exp(scores - row_max)
    attention = expon / jnp.sum(expon, axis=-1, keepdims=True)
    attention_low = attention.astype(jnp.bfloat16)
    grad_values = jnp.einsum(
        "hqk,qhc->khc", attention_low, grad_out, preferred_element_type=jnp.float32
    )
    grad_attention = jnp.einsum(
        "qhc,khc->hqk", grad_out, value_per_head, preferred_element_type=jnp.float32
    )
    inner_sum = jnp.sum(attention * grad_attention, axis=-1, keepdims=True)
    grad_scores = (attention * (grad_attention - inner_sum)).astype(jnp.bfloat16)
    grad_query = (
        jnp.einsum("hqk,khc->qhc", grad_scores, key_heads, preferred_element_type=jnp.float32)
        * inv_root
    )
    return (grad_query, grad_values)


def body(
    hidden,
    query_projection_matrix,
    key_projection_matrix,
    value_projection_matrix,
    adapter_down_maps,
    adapter_up_maps,
    cotangent,
    lengths,
    random_signs_down,
    random_signs_up,
):
    seq_count, seq_len, model_width = hidden.shape
    local_cols = query_projection_matrix.shape[1]
    heads_local = local_cols // HEAD_DIM
    token_matrix = hidden.reshape(seq_count * seq_len, model_width)

    def add_rows(weight_piece):
        return jnp.dot(token_matrix, weight_piece, preferred_element_type=jnp.float32)

    parts_dp = lax.axis_size(DP_AXES)
    local_rows = jnp.concatenate(
        [query_projection_matrix, key_projection_matrix, value_projection_matrix], axis=1
    )
    partner_rows = lax.ppermute(local_rows, "zl", [(0, 1), (1, 0)])
    low_first = lax.axis_index("zl") == 0
    pair_rows = jnp.stack(
        [
            jnp.where(low_first, local_rows, partner_rows),
            jnp.where(low_first, partner_rows, local_rows),
        ]
    )
    all_rows = lax.all_gather(pair_rows, ("x", "y"), axis=1, tiled=False).reshape(
        -1, local_rows.shape[1]
    )
    projected = add_rows(all_rows)
    plain_query = projected[:, :local_cols]
    base_key = projected[:, local_cols : 2 * local_cols]
    plain_value = projected[:, 2 * local_cols :]
    rotary_cosines, rotary_sines = rope_tables(seq_len, HEAD_DIM)
    inner_hidden = jnp.einsum(
        "no,wio->nwi", token_matrix, adapter_down_maps, preferred_element_type=jnp.float32
    ).astype(jnp.bfloat16)
    raised_features = jnp.einsum(
        "kdg,dgj->kdj", inner_hidden, adapter_up_maps, preferred_element_type=jnp.float32
    )
    head_layout = (seq_count, seq_len, heads_local, HEAD_DIM)
    query_per_head = apply_rotary(
        (plain_query + adapter_scale * raised_features[:, 0]).reshape(head_layout),
        rotary_cosines,
        rotary_sines,
    ).astype(jnp.bfloat16)
    key_heads = apply_rotary(base_key.reshape(head_layout), rotary_cosines, rotary_sines).astype(
        jnp.bfloat16
    )
    value_per_head = (
        (plain_value + adapter_scale * raised_features[:, 1])
        .astype(jnp.bfloat16)
        .reshape(head_layout)
    )
    valid = jnp.arange(seq_len, dtype=jnp.int32)[None, :] < lengths[:, None]
    masked_out = jnp.where(valid[:, :, None], cotangent, jnp.zeros_like(cotangent)).reshape(
        head_layout
    )
    grad_query, grad_values = lax.map(
        attention_grads, (query_per_head, key_heads, value_per_head, masked_out, lengths)
    )
    grad_query = (
        unrotate(grad_query, rotary_cosines, rotary_sines)
        .astype(jnp.bfloat16)
        .reshape(seq_count, seq_len, local_cols)
    )
    grad_values = grad_values.astype(jnp.bfloat16).reshape(seq_count, seq_len, local_cols)
    per_head_gradient = jnp.stack([grad_query, grad_values], axis=2)
    branch_portion = jnp.einsum(
        "liov,ohv->lioh", per_head_gradient, adapter_up_maps, preferred_element_type=jnp.float32
    )
    adapter_branch = lax.psum(branch_portion, TP_AXES).astype(jnp.bfloat16)
    middle_seq = inner_hidden.reshape(seq_count, seq_len, 2, ADAPTER_RANK)
    up_map_gradient = adapter_scale * jnp.einsum(
        "esar,esac->earc", middle_seq, per_head_gradient, preferred_element_type=jnp.float32
    )
    parts_tensor = lax.axis_size(TP_AXES)
    row_block = model_width // (parts_dp * parts_tensor)
    hidden_blocks = hidden.reshape(seq_count, seq_len, parts_dp, parts_tensor, row_block)
    local_column_range = lax.dynamic_index_in_dim(
        hidden_blocks, lax.axis_index(TP_AXES), axis=3, keepdims=False
    )
    down_map_local = adapter_scale * jnp.einsum(
        "ykzu,ykhc->yhzuc", adapter_branch, local_column_range, preferred_element_type=jnp.float32
    )
    down_map_local = down_map_local.reshape(seq_count, parts_dp, 1, 2 * ADAPTER_RANK * row_block)
    slice_len = HEAD_DIM // parts_dp
    up_blocks = up_map_gradient.reshape(
        seq_count, 2, ADAPTER_RANK, heads_local, parts_dp, slice_len
    )
    up_blocks = up_blocks.transpose(0, 4, 1, 2, 3, 5).reshape(
        seq_count, parts_dp, 1, 2 * ADAPTER_RANK * heads_local * slice_len
    )
    packed = jnp.concatenate([down_map_local, up_blocks], axis=3).astype(jnp.bfloat16)
    routed = lax.all_to_all(packed, DP_AXES, split_axis=1, concat_axis=0, tiled=True)
    gathered = routed.reshape(routed.shape[0], routed.shape[3])
    down_count = down_map_local.shape[3]
    down_table = random_signs_down.reshape(down_count, random_signs_down.shape[-1])
    up_table = random_signs_up.reshape(gathered.shape[1] - down_count, random_signs_up.shape[-1])
    partial = (
        jnp.dot(gathered[:, :down_count], down_table, preferred_element_type=jnp.float32)
        + jnp.dot(gathered[:, down_count:], up_table, preferred_element_type=jnp.float32)
    ).astype(jnp.bfloat16)
    own_count = partial.shape[0] // parts_dp
    to_owner = lax.all_to_all(
        partial.reshape(parts_dp, own_count, partial.shape[1]), DP_AXES, 0, 0, tiled=True
    )
    own_rows = jnp.sum(to_owner.astype(jnp.float32), axis=0)
    feat_block = own_rows.shape[1] // parts_tensor
    full_rows = lax.psum(own_rows, TP_AXES)
    squares = jnp.sum(full_rows * full_rows, axis=1)
    features_local = lax.dynamic_slice_in_dim(
        full_rows, lax.axis_index(TP_AXES) * feat_block, feat_block, axis=1
    )
    return features_local * lax.rsqrt(squares / FEAT + norm_eps)[:, None]


def solution(mesh):
    fine_mesh = Mesh(mesh.devices.reshape(2, 4, 4, 2, 2), ("zl", "x", "y", "zh", "core"))
    return jax.shard_map(
        body,
        mesh=fine_mesh,
        in_specs=(
            P(DP_AXES, None, None),
            P(DP_AXES, TP_AXES),
            P(DP_AXES, TP_AXES),
            P(DP_AXES, TP_AXES),
            P(),
            P(None, None, TP_AXES),
            P(DP_AXES, None, TP_AXES),
            P(DP_AXES),
            P(None, None, DP_AXES + TP_AXES, None),
            P(None, None, TP_AXES, DP_AXES, None),
        ),
        out_specs=P(DP_AXES, TP_AXES),
        check_vma=False,
    )
```

```python
import jax
import jax.numpy as jnp
from jax import lax
from jax.sharding import Mesh, PartitionSpec as P

HEAD_DIM = 128
ADAPTER_RANK = 8
FEAT = 4096
DP_AXES = ("zl", "x", "y")
TP_AXES = ("zh", "core")


adapter_scale = 2.0
rope_base = 10000.0
norm_eps = 1e-05
masked_score = -1e30


def rope_tables(seq_len, head_width):
    half_width = head_width // 2
    frequency = rope_base ** (-2.0 * jnp.arange(half_width, dtype=jnp.float32) / head_width)
    angles = jnp.arange(seq_len, dtype=jnp.float32)[:, None] * frequency[None, :]
    rotary_cosines = jnp.concatenate([jnp.cos(angles), jnp.cos(angles)], axis=1)
    rotary_sines = jnp.concatenate([jnp.sin(angles), jnp.sin(angles)], axis=1)
    return (rotary_cosines, rotary_sines)


def apply_rotary(tensor_in, rotary_cosines, rotary_sines):
    half_width = tensor_in.shape[-1] // 2
    turned = jnp.concatenate([-tensor_in[..., half_width:], tensor_in[..., :half_width]], axis=-1)
    return tensor_in * rotary_cosines[:, None, :] + turned * rotary_sines[:, None, :]


def unrotate(gradient, rotary_cosines, rotary_sines):
    half_width = gradient.shape[-1] // 2
    scaled = gradient * rotary_sines[:, None, :]
    rotated_back = jnp.concatenate([scaled[..., half_width:], -scaled[..., :half_width]], axis=-1)
    return gradient * rotary_cosines[:, None, :] + rotated_back


def attention_grads(example):
    query_per_head, key_heads, value_per_head, grad_out, seq_length = example
    seq_len = query_per_head.shape[0]
    inv_root = query_per_head.shape[-1] ** (-0.5)
    scores = (
        jnp.einsum("qhc,khc->hqk", query_per_head, key_heads, preferred_element_type=jnp.float32)
        * inv_root
    )
    query_pos = jnp.arange(seq_len, dtype=jnp.int32)[:, None]
    key_pos = jnp.arange(seq_len, dtype=jnp.int32)[None, :]
    allowed = (key_pos <= query_pos) & (key_pos < seq_length)
    scores = jnp.where(allowed[None], scores, masked_score)
    row_max = jnp.max(scores, axis=-1, keepdims=True)
    expon = jnp.exp(scores - row_max)
    attention = expon / jnp.sum(expon, axis=-1, keepdims=True)
    attention_low = attention.astype(jnp.bfloat16)
    grad_values = jnp.einsum(
        "hqk,qhc->khc", attention_low, grad_out, preferred_element_type=jnp.float32
    )
    grad_attention = jnp.einsum(
        "qhc,khc->hqk", grad_out, value_per_head, preferred_element_type=jnp.float32
    )
    inner_sum = jnp.sum(attention * grad_attention, axis=-1, keepdims=True)
    grad_scores = (attention * (grad_attention - inner_sum)).astype(jnp.bfloat16)
    grad_query = (
        jnp.einsum("hqk,khc->qhc", grad_scores, key_heads, preferred_element_type=jnp.float32)
        * inv_root
    )
    return (grad_query, grad_values)


def body(
    hidden,
    query_projection_matrix,
    key_projection_matrix,
    value_projection_matrix,
    adapter_down_maps,
    adapter_up_maps,
    cotangent,
    lengths,
    random_signs_down,
    random_signs_up,
):
    seq_count, seq_len, model_width = hidden.shape
    local_cols = query_projection_matrix.shape[1]
    heads_local = local_cols // HEAD_DIM
    token_matrix = hidden.reshape(seq_count * seq_len, model_width)

    def add_rows(weight_piece):
        return jnp.dot(token_matrix, weight_piece, preferred_element_type=jnp.float32)

    parts_dp = lax.axis_size(DP_AXES)
    local_rows = jnp.concatenate(
        [query_projection_matrix, key_projection_matrix, value_projection_matrix], axis=1
    )
    partner_rows = lax.ppermute(local_rows, "zl", [(0, 1), (1, 0)])
    low_first = lax.axis_index("zl") == 0
    pair_rows = jnp.stack(
        [
            jnp.where(low_first, local_rows, partner_rows),
            jnp.where(low_first, partner_rows, local_rows),
        ]
    )
    all_rows = lax.all_gather(pair_rows, ("x", "y"), axis=1, tiled=False).reshape(
        -1, local_rows.shape[1]
    )
    projected = add_rows(all_rows)
    plain_query = projected[:, :local_cols]
    base_key = projected[:, local_cols : 2 * local_cols]
    plain_value = projected[:, 2 * local_cols :]
    rotary_cosines, rotary_sines = rope_tables(seq_len, HEAD_DIM)
    inner_hidden = jnp.einsum(
        "no,wio->nwi", token_matrix, adapter_down_maps, preferred_element_type=jnp.float32
    ).astype(jnp.bfloat16)
    raised_features = jnp.einsum(
        "kdg,dgj->kdj", inner_hidden, adapter_up_maps, preferred_element_type=jnp.float32
    )
    head_layout = (seq_count, seq_len, heads_local, HEAD_DIM)
    query_per_head = apply_rotary(
        (plain_query + adapter_scale * raised_features[:, 0]).reshape(head_layout),
        rotary_cosines,
        rotary_sines,
    ).astype(jnp.bfloat16)
    key_heads = apply_rotary(base_key.reshape(head_layout), rotary_cosines, rotary_sines).astype(
        jnp.bfloat16
    )
    value_per_head = (
        (plain_value + adapter_scale * raised_features[:, 1])
        .astype(jnp.bfloat16)
        .reshape(head_layout)
    )
    valid = jnp.arange(seq_len, dtype=jnp.int32)[None, :] < lengths[:, None]
    masked_out = jnp.where(valid[:, :, None], cotangent, jnp.zeros_like(cotangent)).reshape(
        head_layout
    )
    grad_query, grad_values = jax.vmap(attention_grads)(
        (query_per_head, key_heads, value_per_head, masked_out, lengths)
    )
    grad_query = (
        unrotate(grad_query, rotary_cosines, rotary_sines)
        .astype(jnp.bfloat16)
        .reshape(seq_count, seq_len, local_cols)
    )
    grad_values = grad_values.astype(jnp.bfloat16).reshape(seq_count, seq_len, local_cols)
    per_head_gradient = jnp.stack([grad_query, grad_values], axis=2)
    branch_portion = jnp.einsum(
        "liov,ohv->lioh", per_head_gradient, adapter_up_maps, preferred_element_type=jnp.float32
    )
    adapter_branch = lax.psum(branch_portion, TP_AXES).astype(jnp.bfloat16)
    middle_seq = inner_hidden.reshape(seq_count, seq_len, 2, ADAPTER_RANK)
    up_map_gradient = adapter_scale * jnp.einsum(
        "esar,esac->earc", middle_seq, per_head_gradient, preferred_element_type=jnp.float32
    )
    parts_tensor = lax.axis_size(TP_AXES)
    row_block = model_width // (parts_dp * parts_tensor)
    hidden_blocks = hidden.reshape(seq_count, seq_len, parts_dp, parts_tensor, row_block)
    local_column_range = lax.dynamic_index_in_dim(
        hidden_blocks, lax.axis_index(TP_AXES), axis=3, keepdims=False
    )
    down_map_local = adapter_scale * jnp.einsum(
        "ykzu,ykhc->yhzuc", adapter_branch, local_column_range, preferred_element_type=jnp.float32
    )
    down_map_local = down_map_local.reshape(seq_count, parts_dp, 1, 2 * ADAPTER_RANK * row_block)
    slice_len = HEAD_DIM // parts_dp
    up_blocks = up_map_gradient.reshape(
        seq_count, 2, ADAPTER_RANK, heads_local, parts_dp, slice_len
    )
    up_blocks = up_blocks.transpose(0, 4, 1, 2, 3, 5).reshape(
        seq_count, parts_dp, 1, 2 * ADAPTER_RANK * heads_local * slice_len
    )
    packed = jnp.concatenate([down_map_local, up_blocks], axis=3).astype(jnp.bfloat16)
    routed = lax.all_to_all(packed, DP_AXES, split_axis=1, concat_axis=0, tiled=True)
    gathered = routed.reshape(routed.shape[0], routed.shape[3])
    down_count = down_map_local.shape[3]
    down_table = random_signs_down.reshape(down_count, random_signs_down.shape[-1])
    up_table = random_signs_up.reshape(gathered.shape[1] - down_count, random_signs_up.shape[-1])
    partial = (
        jnp.dot(gathered[:, :down_count], down_table, preferred_element_type=jnp.float32)
        + jnp.dot(gathered[:, down_count:], up_table, preferred_element_type=jnp.float32)
    ).astype(jnp.bfloat16)
    own_count = partial.shape[0] // parts_dp
    to_owner = lax.all_to_all(
        partial.reshape(parts_dp, own_count, partial.shape[1]), DP_AXES, 0, 0, tiled=True
    )
    own_rows = jnp.sum(to_owner.astype(jnp.float32), axis=0)
    feat_block = own_rows.shape[1] // parts_tensor
    full_rows = lax.psum(own_rows, TP_AXES)
    squares = jnp.sum(full_rows * full_rows, axis=1)
    features_local = lax.dynamic_slice_in_dim(
        full_rows, lax.axis_index(TP_AXES) * feat_block, feat_block, axis=1
    )
    return features_local * lax.rsqrt(squares / FEAT + norm_eps)[:, None]


def solution(mesh):
    fine_mesh = Mesh(mesh.devices.reshape(2, 4, 4, 2, 2), ("zl", "x", "y", "zh", "core"))
    return jax.shard_map(
        body,
        mesh=fine_mesh,
        in_specs=(
            P(DP_AXES, None, None),
            P(DP_AXES, TP_AXES),
            P(DP_AXES, TP_AXES),
            P(DP_AXES, TP_AXES),
            P(),
            P(None, None, TP_AXES),
            P(DP_AXES, None, TP_AXES),
            P(DP_AXES),
            P(None, None, DP_AXES + TP_AXES, None),
            P(None, None, TP_AXES, DP_AXES, None),
        ),
        out_specs=P(DP_AXES, TP_AXES),
        check_vma=False,
    )
```

```python
import jax
import jax.numpy as jnp
from jax import lax
from jax.sharding import Mesh, PartitionSpec as P

HEAD_DIM = 128
ADAPTER_RANK = 8
FEAT = 4096
DP_AXES = ("zl", "x", "y")
TP_AXES = ("zh", "core")


adapter_scale = 2.0
rope_base = 10000.0
norm_eps = 1e-05
masked_score = -1e30


def rope_tables(seq_len, head_width):
    half_width = head_width // 2
    frequency = rope_base ** (-2.0 * jnp.arange(half_width, dtype=jnp.float32) / head_width)
    angles = jnp.arange(seq_len, dtype=jnp.float32)[:, None] * frequency[None, :]
    rotary_cosines = jnp.concatenate([jnp.cos(angles), jnp.cos(angles)], axis=1)
    rotary_sines = jnp.concatenate([jnp.sin(angles), jnp.sin(angles)], axis=1)
    return (rotary_cosines, rotary_sines)


def apply_rotary(tensor_in, rotary_cosines, rotary_sines):
    half_width = tensor_in.shape[-1] // 2
    turned = jnp.concatenate([-tensor_in[..., half_width:], tensor_in[..., :half_width]], axis=-1)
    return tensor_in * rotary_cosines[:, None, :] + turned * rotary_sines[:, None, :]


def unrotate(gradient, rotary_cosines, rotary_sines):
    half_width = gradient.shape[-1] // 2
    scaled = gradient * rotary_sines[:, None, :]
    rotated_back = jnp.concatenate([scaled[..., half_width:], -scaled[..., :half_width]], axis=-1)
    return gradient * rotary_cosines[:, None, :] + rotated_back


def attention_grads(example):
    query_per_head, key_heads, value_per_head, grad_out, seq_length = example
    seq_len = query_per_head.shape[0]
    inv_root = query_per_head.shape[-1] ** (-0.5)
    scores = (
        jnp.einsum("qhc,khc->hqk", query_per_head, key_heads, preferred_element_type=jnp.float32)
        * inv_root
    )
    query_pos = jnp.arange(seq_len, dtype=jnp.int32)[:, None]
    key_pos = jnp.arange(seq_len, dtype=jnp.int32)[None, :]
    allowed = (key_pos <= query_pos) & (key_pos < seq_length)
    scores = jnp.where(allowed[None], scores, masked_score)
    row_max = jnp.max(scores, axis=-1, keepdims=True)
    expon = jnp.exp(scores - row_max)
    attention = expon / jnp.sum(expon, axis=-1, keepdims=True)
    attention_low = attention.astype(jnp.bfloat16)
    grad_values = jnp.einsum(
        "hqk,qhc->khc", attention_low, grad_out, preferred_element_type=jnp.float32
    )
    grad_attention = jnp.einsum(
        "qhc,khc->hqk", grad_out, value_per_head, preferred_element_type=jnp.float32
    )
    inner_sum = jnp.sum(attention * grad_attention, axis=-1, keepdims=True)
    grad_scores = (attention * (grad_attention - inner_sum)).astype(jnp.bfloat16)
    grad_query = (
        jnp.einsum("hqk,khc->qhc", grad_scores, key_heads, preferred_element_type=jnp.float32)
        * inv_root
    )
    return (grad_query, grad_values)


def body(
    hidden,
    query_projection_matrix,
    key_projection_matrix,
    value_projection_matrix,
    adapter_down_maps,
    adapter_up_maps,
    cotangent,
    lengths,
    random_signs_down,
    random_signs_up,
):
    seq_count, seq_len, model_width = hidden.shape
    local_cols = query_projection_matrix.shape[1]
    heads_local = local_cols // HEAD_DIM
    token_matrix = hidden.reshape(seq_count * seq_len, model_width)

    def add_rows(weight_piece):
        return jnp.dot(token_matrix, weight_piece, preferred_element_type=jnp.float32)

    parts_dp = lax.axis_size(DP_AXES)
    local_rows = jnp.concatenate(
        [query_projection_matrix, key_projection_matrix, value_projection_matrix], axis=1
    )
    partner_rows = lax.ppermute(local_rows, "zl", [(0, 1), (1, 0)])
    low_first = lax.axis_index("zl") == 0
    pair_rows = jnp.stack(
        [
            jnp.where(low_first, local_rows, partner_rows),
            jnp.where(low_first, partner_rows, local_rows),
        ]
    )
    all_rows = lax.all_gather(pair_rows, ("x", "y"), axis=1, tiled=False).reshape(
        -1, local_rows.shape[1]
    )
    projected = add_rows(all_rows)
    plain_query = projected[:, :local_cols]
    base_key = projected[:, local_cols : 2 * local_cols]
    plain_value = projected[:, 2 * local_cols :]
    rotary_cosines, rotary_sines = rope_tables(seq_len, HEAD_DIM)
    inner_hidden = jnp.einsum(
        "no,wio->nwi", token_matrix, adapter_down_maps, preferred_element_type=jnp.float32
    ).astype(jnp.bfloat16)
    raised_features = jnp.einsum(
        "kdg,dgj->kdj", inner_hidden, adapter_up_maps, preferred_element_type=jnp.float32
    )
    head_layout = (seq_count, seq_len, heads_local, HEAD_DIM)
    query_per_head = apply_rotary(
        (plain_query + adapter_scale * raised_features[:, 0]).reshape(head_layout),
        rotary_cosines,
        rotary_sines,
    ).astype(jnp.bfloat16)
    key_heads = apply_rotary(base_key.reshape(head_layout), rotary_cosines, rotary_sines).astype(
        jnp.bfloat16
    )
    value_per_head = (
        (plain_value + adapter_scale * raised_features[:, 1])
        .astype(jnp.bfloat16)
        .reshape(head_layout)
    )
    valid = jnp.arange(seq_len, dtype=jnp.int32)[None, :] < lengths[:, None]
    masked_out = jnp.where(valid[:, :, None], cotangent, jnp.zeros_like(cotangent)).reshape(
        head_layout
    )
    grad_query, grad_values = lax.map(
        attention_grads, (query_per_head, key_heads, value_per_head, masked_out, lengths)
    )
    grad_query = (
        unrotate(grad_query, rotary_cosines, rotary_sines)
        .astype(jnp.bfloat16)
        .reshape(seq_count, seq_len, local_cols)
    )
    grad_values = grad_values.astype(jnp.bfloat16).reshape(seq_count, seq_len, local_cols)
    per_head_gradient = jnp.stack([grad_query, grad_values], axis=2)
    branch_portion = jnp.einsum(
        "liov,ohv->lioh", per_head_gradient, adapter_up_maps, preferred_element_type=jnp.float32
    )
    adapter_branch = lax.psum(branch_portion, TP_AXES).astype(jnp.bfloat16)
    middle_seq = inner_hidden.reshape(seq_count, seq_len, 2, ADAPTER_RANK)
    up_map_gradient = adapter_scale * jnp.einsum(
        "esar,esac->earc", middle_seq, per_head_gradient, preferred_element_type=jnp.float32
    )
    parts_tensor = lax.axis_size(TP_AXES)
    row_block = model_width // (parts_dp * parts_tensor)
    hidden_blocks = hidden.reshape(seq_count, seq_len, parts_dp, parts_tensor, row_block)
    local_column_range = lax.dynamic_index_in_dim(
        hidden_blocks, lax.axis_index(TP_AXES), axis=3, keepdims=False
    )
    down_map_local = adapter_scale * jnp.einsum(
        "ykzu,ykhc->yhzuc", adapter_branch, local_column_range, preferred_element_type=jnp.float32
    )
    down_map_local = down_map_local.reshape(seq_count, parts_dp, 1, 2 * ADAPTER_RANK * row_block)
    slice_len = HEAD_DIM // parts_dp
    up_blocks = up_map_gradient.reshape(
        seq_count, 2, ADAPTER_RANK, heads_local, parts_dp, slice_len
    )
    up_blocks = up_blocks.transpose(0, 4, 1, 2, 3, 5).reshape(
        seq_count, parts_dp, 1, 2 * ADAPTER_RANK * heads_local * slice_len
    )
    packed = jnp.concatenate([down_map_local, up_blocks], axis=3).astype(jnp.bfloat16)
    routed = lax.all_to_all(packed, DP_AXES, split_axis=1, concat_axis=0, tiled=True)
    gathered = routed.reshape(routed.shape[0], routed.shape[3])
    down_count = down_map_local.shape[3]
    down_table = random_signs_down.reshape(down_count, random_signs_down.shape[-1])
    up_table = random_signs_up.reshape(gathered.shape[1] - down_count, random_signs_up.shape[-1])
    partial = (
        jnp.dot(gathered[:, :down_count], down_table, preferred_element_type=jnp.float32)
        + jnp.dot(gathered[:, down_count:], up_table, preferred_element_type=jnp.float32)
    ).astype(jnp.bfloat16)
    own_count = partial.shape[0] // parts_dp
    feat_block = partial.shape[1] // parts_tensor
    blocks = partial.reshape(parts_dp, own_count, parts_tensor, feat_block).transpose(0, 2, 1, 3)
    to_owner = lax.all_to_all(
        blocks.reshape(parts_dp * parts_tensor, own_count, feat_block),
        DP_AXES + TP_AXES,
        0,
        0,
        tiled=True,
    )
    features_local = jnp.sum(to_owner.astype(jnp.float32), axis=0)
    squares = lax.psum(jnp.sum(features_local * features_local, axis=1), TP_AXES)
    return features_local * lax.rsqrt(squares / FEAT + norm_eps)[:, None]


def solution(mesh):
    fine_mesh = Mesh(mesh.devices.reshape(2, 4, 4, 2, 2), ("zl", "x", "y", "zh", "core"))
    return jax.shard_map(
        body,
        mesh=fine_mesh,
        in_specs=(
            P(DP_AXES, None, None),
            P(DP_AXES, TP_AXES),
            P(DP_AXES, TP_AXES),
            P(DP_AXES, TP_AXES),
            P(),
            P(None, None, TP_AXES),
            P(DP_AXES, None, TP_AXES),
            P(DP_AXES),
            P(None, None, DP_AXES + TP_AXES, None),
            P(None, None, TP_AXES, DP_AXES, None),
        ),
        out_specs=P(DP_AXES, TP_AXES),
        check_vma=False,
    )
```

```python
import jax
import jax.numpy as jnp
from jax import lax
from jax.sharding import Mesh, PartitionSpec as P

HEAD_DIM = 128
ADAPTER_RANK = 8
FEAT = 4096
DP_AXES = ("zl", "x", "y")
TP_AXES = ("zh", "core")


adapter_scale = 2.0
rope_base = 10000.0
norm_eps = 1e-05
masked_score = -1e30


def rope_tables(seq_len, head_width):
    half_width = head_width // 2
    frequency = rope_base ** (-2.0 * jnp.arange(half_width, dtype=jnp.float32) / head_width)
    angles = jnp.arange(seq_len, dtype=jnp.float32)[:, None] * frequency[None, :]
    rotary_cosines = jnp.concatenate([jnp.cos(angles), jnp.cos(angles)], axis=1)
    rotary_sines = jnp.concatenate([jnp.sin(angles), jnp.sin(angles)], axis=1)
    return (rotary_cosines, rotary_sines)


def apply_rotary(tensor_in, rotary_cosines, rotary_sines):
    half_width = tensor_in.shape[-1] // 2
    turned = jnp.concatenate([-tensor_in[..., half_width:], tensor_in[..., :half_width]], axis=-1)
    return tensor_in * rotary_cosines[:, None, :] + turned * rotary_sines[:, None, :]


def unrotate(gradient, rotary_cosines, rotary_sines):
    half_width = gradient.shape[-1] // 2
    scaled = gradient * rotary_sines[:, None, :]
    rotated_back = jnp.concatenate([scaled[..., half_width:], -scaled[..., :half_width]], axis=-1)
    return gradient * rotary_cosines[:, None, :] + rotated_back


def attention_grads(example):
    query_per_head, key_heads, value_per_head, grad_out, seq_length = example
    seq_len = query_per_head.shape[0]
    inv_root = query_per_head.shape[-1] ** (-0.5)
    scores = (
        jnp.einsum("qhc,khc->hqk", query_per_head, key_heads, preferred_element_type=jnp.float32)
        * inv_root
    )
    query_pos = jnp.arange(seq_len, dtype=jnp.int32)[:, None]
    key_pos = jnp.arange(seq_len, dtype=jnp.int32)[None, :]
    allowed = (key_pos <= query_pos) & (key_pos < seq_length)
    scores = jnp.where(allowed[None], scores, masked_score)
    row_max = jnp.max(scores, axis=-1, keepdims=True)
    expon = jnp.exp(scores - row_max)
    attention = expon / jnp.sum(expon, axis=-1, keepdims=True)
    attention_low = attention.astype(jnp.bfloat16)
    grad_values = jnp.einsum(
        "hqk,qhc->khc", attention_low, grad_out, preferred_element_type=jnp.float32
    )
    grad_attention = jnp.einsum(
        "qhc,khc->hqk", grad_out, value_per_head, preferred_element_type=jnp.float32
    )
    inner_sum = jnp.sum(attention * grad_attention, axis=-1, keepdims=True)
    grad_scores = (attention * (grad_attention - inner_sum)).astype(jnp.bfloat16)
    grad_query = (
        jnp.einsum("hqk,khc->qhc", grad_scores, key_heads, preferred_element_type=jnp.float32)
        * inv_root
    )
    return (grad_query, grad_values)


def body(
    hidden,
    query_projection_matrix,
    key_projection_matrix,
    value_projection_matrix,
    adapter_down_maps,
    adapter_up_maps,
    cotangent,
    lengths,
    random_signs_down,
    random_signs_up,
):
    seq_count, seq_len, model_width = hidden.shape
    local_cols = query_projection_matrix.shape[1]
    heads_local = local_cols // HEAD_DIM
    token_matrix = hidden.reshape(seq_count * seq_len, model_width)

    def add_rows(weight_piece):
        return jnp.dot(token_matrix, weight_piece, preferred_element_type=jnp.float32)

    parts_dp = lax.axis_size(DP_AXES)
    local_rows = jnp.concatenate(
        [query_projection_matrix, key_projection_matrix, value_projection_matrix], axis=1
    )
    partner_rows = lax.ppermute(local_rows, "zl", [(0, 1), (1, 0)])
    low_first = lax.axis_index("zl") == 0
    pair_rows = jnp.stack(
        [
            jnp.where(low_first, local_rows, partner_rows),
            jnp.where(low_first, partner_rows, local_rows),
        ]
    )
    all_rows = lax.all_gather(pair_rows, ("x", "y"), axis=1, tiled=False).reshape(
        -1, local_rows.shape[1]
    )
    projected = add_rows(all_rows)
    plain_query = projected[:, :local_cols]
    base_key = projected[:, local_cols : 2 * local_cols]
    plain_value = projected[:, 2 * local_cols :]
    rotary_cosines, rotary_sines = rope_tables(seq_len, HEAD_DIM)
    inner_hidden = jnp.einsum(
        "no,wio->nwi", token_matrix, adapter_down_maps, preferred_element_type=jnp.float32
    ).astype(jnp.bfloat16)
    raised_features = jnp.einsum(
        "kdg,dgj->kdj", inner_hidden, adapter_up_maps, preferred_element_type=jnp.float32
    )
    head_layout = (seq_count, seq_len, heads_local, HEAD_DIM)
    query_per_head = apply_rotary(
        (plain_query + adapter_scale * raised_features[:, 0]).reshape(head_layout),
        rotary_cosines,
        rotary_sines,
    ).astype(jnp.bfloat16)
    key_heads = apply_rotary(base_key.reshape(head_layout), rotary_cosines, rotary_sines).astype(
        jnp.bfloat16
    )
    value_per_head = (
        (plain_value + adapter_scale * raised_features[:, 1])
        .astype(jnp.bfloat16)
        .reshape(head_layout)
    )
    valid = jnp.arange(seq_len, dtype=jnp.int32)[None, :] < lengths[:, None]
    masked_out = jnp.where(valid[:, :, None], cotangent, jnp.zeros_like(cotangent)).reshape(
        head_layout
    )
    grad_query, grad_values = lax.map(
        attention_grads, (query_per_head, key_heads, value_per_head, masked_out, lengths)
    )
    grad_query = (
        unrotate(grad_query, rotary_cosines, rotary_sines)
        .astype(jnp.bfloat16)
        .reshape(seq_count, seq_len, local_cols)
    )
    grad_values = grad_values.astype(jnp.bfloat16).reshape(seq_count, seq_len, local_cols)
    per_head_gradient = jnp.stack([grad_query, grad_values], axis=2)
    branch_portion = jnp.einsum(
        "liov,ohv->lioh", per_head_gradient, adapter_up_maps, preferred_element_type=jnp.float32
    )
    adapter_branch = jnp.sum(
        lax.all_gather(branch_portion, TP_AXES, axis=0, tiled=False), axis=0
    ).astype(jnp.bfloat16)
    middle_seq = inner_hidden.reshape(seq_count, seq_len, 2, ADAPTER_RANK)
    up_map_gradient = adapter_scale * jnp.einsum(
        "esar,esac->earc", middle_seq, per_head_gradient, preferred_element_type=jnp.float32
    )
    parts_tensor = lax.axis_size(TP_AXES)
    row_block = model_width // (parts_dp * parts_tensor)
    hidden_blocks = hidden.reshape(seq_count, seq_len, parts_dp, parts_tensor, row_block)
    local_column_range = lax.dynamic_index_in_dim(
        hidden_blocks, lax.axis_index(TP_AXES), axis=3, keepdims=False
    )
    down_map_local = adapter_scale * jnp.einsum(
        "ykzu,ykhc->yhzuc", adapter_branch, local_column_range, preferred_element_type=jnp.float32
    )
    down_map_local = down_map_local.reshape(seq_count, parts_dp, 1, 2 * ADAPTER_RANK * row_block)
    slice_len = HEAD_DIM // parts_dp
    up_blocks = up_map_gradient.reshape(
        seq_count, 2, ADAPTER_RANK, heads_local, parts_dp, slice_len
    )
    up_blocks = up_blocks.transpose(0, 4, 1, 2, 3, 5).reshape(
        seq_count, parts_dp, 1, 2 * ADAPTER_RANK * heads_local * slice_len
    )
    packed = jnp.concatenate([down_map_local, up_blocks], axis=3).astype(jnp.bfloat16)
    routed = lax.all_to_all(packed, DP_AXES, split_axis=1, concat_axis=0, tiled=True)
    gathered = routed.reshape(routed.shape[0], routed.shape[3])
    down_count = down_map_local.shape[3]
    down_table = random_signs_down.reshape(down_count, random_signs_down.shape[-1])
    up_table = random_signs_up.reshape(gathered.shape[1] - down_count, random_signs_up.shape[-1])
    partial = (
        jnp.dot(gathered[:, :down_count], down_table, preferred_element_type=jnp.float32)
        + jnp.dot(gathered[:, down_count:], up_table, preferred_element_type=jnp.float32)
    ).astype(jnp.bfloat16)
    own_count = partial.shape[0] // parts_dp
    feat_block = partial.shape[1] // parts_tensor
    blocks = partial.reshape(parts_dp, own_count, parts_tensor, feat_block).transpose(0, 2, 1, 3)
    to_owner = lax.all_to_all(
        blocks.reshape(parts_dp * parts_tensor, own_count, feat_block),
        DP_AXES + TP_AXES,
        0,
        0,
        tiled=True,
    )
    features_local = jnp.sum(to_owner.astype(jnp.float32), axis=0)
    squares = lax.psum(jnp.sum(features_local * features_local, axis=1), TP_AXES)
    return features_local * lax.rsqrt(squares / FEAT + norm_eps)[:, None]


def solution(mesh):
    fine_mesh = Mesh(mesh.devices.reshape(2, 4, 4, 2, 2), ("zl", "x", "y", "zh", "core"))
    return jax.shard_map(
        body,
        mesh=fine_mesh,
        in_specs=(
            P(DP_AXES, None, None),
            P(DP_AXES, TP_AXES),
            P(DP_AXES, TP_AXES),
            P(DP_AXES, TP_AXES),
            P(),
            P(None, None, TP_AXES),
            P(DP_AXES, None, TP_AXES),
            P(DP_AXES),
            P(None, None, DP_AXES + TP_AXES, None),
            P(None, None, TP_AXES, DP_AXES, None),
        ),
        out_specs=P(DP_AXES, TP_AXES),
        check_vma=False,
    )
```

```python
import jax
import jax.numpy as jnp
from jax import lax
from jax.sharding import Mesh, PartitionSpec as P

HEAD_DIM = 128
ADAPTER_RANK = 8
FEAT = 4096
DP_AXES = ("zl", "x", "y")
TP_AXES = ("zh", "core")


adapter_scale = 2.0
rope_base = 10000.0
norm_eps = 1e-05
masked_score = -1e30


def rope_tables(seq_len, head_width):
    half_width = head_width // 2
    frequency = rope_base ** (-2.0 * jnp.arange(half_width, dtype=jnp.float32) / head_width)
    angles = jnp.arange(seq_len, dtype=jnp.float32)[:, None] * frequency[None, :]
    rotary_cosines = jnp.concatenate([jnp.cos(angles), jnp.cos(angles)], axis=1)
    rotary_sines = jnp.concatenate([jnp.sin(angles), jnp.sin(angles)], axis=1)
    return (rotary_cosines, rotary_sines)


def apply_rotary(tensor_in, rotary_cosines, rotary_sines):
    half_width = tensor_in.shape[-1] // 2
    turned = jnp.concatenate([-tensor_in[..., half_width:], tensor_in[..., :half_width]], axis=-1)
    return tensor_in * rotary_cosines[:, None, :] + turned * rotary_sines[:, None, :]


def unrotate(gradient, rotary_cosines, rotary_sines):
    half_width = gradient.shape[-1] // 2
    scaled = gradient * rotary_sines[:, None, :]
    rotated_back = jnp.concatenate([scaled[..., half_width:], -scaled[..., :half_width]], axis=-1)
    return gradient * rotary_cosines[:, None, :] + rotated_back


def attention_grads(example):
    query_per_head, key_heads, value_per_head, grad_out, seq_length = example
    seq_len = query_per_head.shape[0]
    inv_root = query_per_head.shape[-1] ** (-0.5)
    scores = (
        jnp.einsum("qhc,khc->hqk", query_per_head, key_heads, preferred_element_type=jnp.float32)
        * inv_root
    )
    query_pos = jnp.arange(seq_len, dtype=jnp.int32)[:, None]
    key_pos = jnp.arange(seq_len, dtype=jnp.int32)[None, :]
    allowed = (key_pos <= query_pos) & (key_pos < seq_length)
    scores = jnp.where(allowed[None], scores, masked_score)
    row_max = jnp.max(scores, axis=-1, keepdims=True)
    expon = jnp.exp(scores - row_max)
    attention = expon / jnp.sum(expon, axis=-1, keepdims=True)
    attention_low = attention.astype(jnp.bfloat16)
    grad_values = jnp.einsum(
        "hqk,qhc->khc", attention_low, grad_out, preferred_element_type=jnp.float32
    )
    grad_attention = jnp.einsum(
        "qhc,khc->hqk", grad_out, value_per_head, preferred_element_type=jnp.float32
    )
    inner_sum = jnp.sum(attention * grad_attention, axis=-1, keepdims=True)
    grad_scores = (attention * (grad_attention - inner_sum)).astype(jnp.bfloat16)
    grad_query = (
        jnp.einsum("hqk,khc->qhc", grad_scores, key_heads, preferred_element_type=jnp.float32)
        * inv_root
    )
    return (grad_query, grad_values)


def body(
    hidden,
    query_projection_matrix,
    key_projection_matrix,
    value_projection_matrix,
    adapter_down_maps,
    adapter_up_maps,
    cotangent,
    lengths,
    random_signs_down,
    random_signs_up,
):
    seq_count, seq_len, model_width = hidden.shape
    local_cols = query_projection_matrix.shape[1]
    heads_local = local_cols // HEAD_DIM
    token_matrix = hidden.reshape(seq_count * seq_len, model_width)

    def add_rows(weight_piece):
        return jnp.dot(token_matrix, weight_piece, preferred_element_type=jnp.float32)

    parts_dp = lax.axis_size(DP_AXES)
    local_rows = jnp.concatenate(
        [query_projection_matrix, key_projection_matrix, value_projection_matrix], axis=1
    )
    partner_rows = lax.ppermute(local_rows, "zl", [(0, 1), (1, 0)])
    low_first = lax.axis_index("zl") == 0
    pair_rows = jnp.stack(
        [
            jnp.where(low_first, local_rows, partner_rows),
            jnp.where(low_first, partner_rows, local_rows),
        ]
    )
    all_rows = lax.all_gather(pair_rows, ("x", "y"), axis=1, tiled=False).reshape(
        -1, local_rows.shape[1]
    )
    projected = add_rows(all_rows)
    plain_query = projected[:, :local_cols]
    base_key = projected[:, local_cols : 2 * local_cols]
    plain_value = projected[:, 2 * local_cols :]
    rotary_cosines, rotary_sines = rope_tables(seq_len, HEAD_DIM)
    inner_hidden = jnp.einsum(
        "no,wio->nwi", token_matrix, adapter_down_maps, preferred_element_type=jnp.float32
    ).astype(jnp.bfloat16)
    raised_features = jnp.einsum(
        "kdg,dgj->kdj", inner_hidden, adapter_up_maps, preferred_element_type=jnp.float32
    )
    head_layout = (seq_count, seq_len, heads_local, HEAD_DIM)
    query_per_head = apply_rotary(
        (plain_query + adapter_scale * raised_features[:, 0]).reshape(head_layout),
        rotary_cosines,
        rotary_sines,
    ).astype(jnp.bfloat16)
    key_heads = apply_rotary(base_key.reshape(head_layout), rotary_cosines, rotary_sines).astype(
        jnp.bfloat16
    )
    value_per_head = (
        (plain_value + adapter_scale * raised_features[:, 1])
        .astype(jnp.bfloat16)
        .reshape(head_layout)
    )
    valid = jnp.arange(seq_len, dtype=jnp.int32)[None, :] < lengths[:, None]
    masked_out = jnp.where(valid[:, :, None], cotangent, jnp.zeros_like(cotangent)).reshape(
        head_layout
    )
    grad_query, grad_values = lax.map(
        attention_grads, (query_per_head, key_heads, value_per_head, masked_out, lengths)
    )
    grad_query = (
        unrotate(grad_query, rotary_cosines, rotary_sines)
        .astype(jnp.bfloat16)
        .reshape(seq_count, seq_len, local_cols)
    )
    grad_values = grad_values.astype(jnp.bfloat16).reshape(seq_count, seq_len, local_cols)
    per_head_gradient = jnp.stack([grad_query, grad_values], axis=2)
    branch_portion = jnp.einsum(
        "liov,ohv->lioh", per_head_gradient, adapter_up_maps, preferred_element_type=jnp.float32
    )
    adapter_branch = jnp.sum(
        lax.all_gather(branch_portion, TP_AXES, axis=0, tiled=False), axis=0
    ).astype(jnp.bfloat16)
    middle_seq = inner_hidden.reshape(seq_count, seq_len, 2, ADAPTER_RANK)
    up_map_gradient = adapter_scale * jnp.einsum(
        "esar,esac->earc", middle_seq, per_head_gradient, preferred_element_type=jnp.float32
    )
    parts_tensor = lax.axis_size(TP_AXES)
    row_block = model_width // (parts_dp * parts_tensor)
    hidden_blocks = hidden.reshape(seq_count, seq_len, parts_dp, parts_tensor, row_block)
    local_column_range = lax.dynamic_index_in_dim(
        hidden_blocks, lax.axis_index(TP_AXES), axis=3, keepdims=False
    )
    down_map_local = adapter_scale * jnp.einsum(
        "ykzu,ykhc->yhzuc", adapter_branch, local_column_range, preferred_element_type=jnp.float32
    )
    down_map_local = down_map_local.reshape(seq_count, parts_dp, 1, 2 * ADAPTER_RANK * row_block)
    slice_len = HEAD_DIM // parts_dp
    up_blocks = up_map_gradient.reshape(
        seq_count, 2, ADAPTER_RANK, heads_local, parts_dp, slice_len
    )
    up_blocks = up_blocks.transpose(0, 4, 1, 2, 3, 5).reshape(
        seq_count, parts_dp, 1, 2 * ADAPTER_RANK * heads_local * slice_len
    )
    packed = jnp.concatenate([down_map_local, up_blocks], axis=3).astype(jnp.bfloat16)
    routed = lax.all_to_all(packed, DP_AXES, split_axis=1, concat_axis=0, tiled=True)
    gathered = routed.reshape(routed.shape[0], routed.shape[3])
    down_count = down_map_local.shape[3]
    down_table = random_signs_down.reshape(down_count, random_signs_down.shape[-1])
    up_table = random_signs_up.reshape(gathered.shape[1] - down_count, random_signs_up.shape[-1])
    partial = (
        jnp.dot(gathered[:, :down_count], down_table, preferred_element_type=jnp.float32)
        + jnp.dot(gathered[:, down_count:], up_table, preferred_element_type=jnp.float32)
    ).astype(jnp.bfloat16)
    own_count = partial.shape[0] // parts_dp
    feat_block = partial.shape[1] // parts_tensor
    blocks = partial.reshape(parts_dp, own_count, parts_tensor, feat_block).transpose(0, 2, 1, 3)
    to_owner = lax.all_to_all(
        blocks.reshape(parts_dp * parts_tensor, own_count, feat_block),
        DP_AXES + TP_AXES,
        0,
        0,
        tiled=True,
    )
    features_local = jnp.sum(to_owner.astype(jnp.float32), axis=0)
    squares = jnp.sum(
        lax.all_gather(jnp.sum(features_local * features_local, axis=1), TP_AXES), axis=0
    )
    return features_local * lax.rsqrt(squares / FEAT + norm_eps)[:, None]


def solution(mesh):
    fine_mesh = Mesh(mesh.devices.reshape(2, 4, 4, 2, 2), ("zl", "x", "y", "zh", "core"))
    return jax.shard_map(
        body,
        mesh=fine_mesh,
        in_specs=(
            P(DP_AXES, None, None),
            P(DP_AXES, TP_AXES),
            P(DP_AXES, TP_AXES),
            P(DP_AXES, TP_AXES),
            P(),
            P(None, None, TP_AXES),
            P(DP_AXES, None, TP_AXES),
            P(DP_AXES),
            P(None, None, DP_AXES + TP_AXES, None),
            P(None, None, TP_AXES, DP_AXES, None),
        ),
        out_specs=P(DP_AXES, TP_AXES),
        check_vma=False,
    )
```
